32 devices in a mesh: grp: 2 (over y), lat: 4 (over z), freq: 4 (over x, core).
Axes of the slice: x: 2, y: 2, z: 4, core: 2. Of those that a mesh axis runs over, the one named last changes fastest.
Arguments:
- source_field: bfloat16 [4, 4, 2304, 512], P('grp', 'freq', 'lat'), parts along dimension 0, may hold values from -6 to 6
- data_field: bfloat16 [4, 4, 2304, 512], P('grp', 'freq', 'lat'), parts along dimension 0, may hold values from -6 to 6
- propagator: bfloat16 [4, 2, 4, 2304, 1152], P('grp', None, 'freq', 'lat'), parts along dimension 0, may hold values from -0.125 to 0.125
- band_start: int32 [4, 4], P('grp', 'lat'), parts along dimension 0, may hold values from 0 to 576, as said below
- freq_slot: int32 [4], P('freq'), may hold values from 0 to 63, as said below
Outputs:
- reflectivity: bfloat16 [4, 2304, 576], P('grp', 'lat'), parts along dimension 0
- source_out: bfloat16 [4, 4, 2304, 512], P('grp', 'freq', 'lat'), parts along dimension 0
- data_out: bfloat16 [4, 4, 2304, 512], P('grp', 'freq', 'lat'), parts along dimension 0
The draws below stay inside these ranges and needn't reach their ends.
There are 2 independent parts, one for each index of `grp`. The reference program is written for one: setup_inputs(seed, part) draws one part's arguments, and reference() takes and returns one part's arrays. A program takes and returns all parts, laid end to end along the dimension named above; an argument that names none is the same for every part. Nothing has to cross between parts.
Inputs may be any that keep to these rules, and one draw needn't show every extreme that they name: `band_start`: every level has one tile whose band starts at 0 and one whose band starts at 576. `freq_slot`: the values are distinct, each block of 16 consecutive values holds exactly one, and both the least and the largest value occur.
All inputs are finite; a program needn't handle non-finite values.
Results may differ from the reference program's by a relative error of at most 0.0092.
Values may be sent and summed in bfloat16 or wider, within the bound.
A program may use at most 64 MiB of HBM per device.

```python
import math
import jax
import jax.numpy as jnp
from jax import lax

TILE = 576
BAND = 1152
SHOTS = 512
LEVELS = 2
FREQS = 4
TILES = 4
NX = 2304


def draw_band_start(key, part):
    starts = jax.random.randint(jax.random.fold_in(key, 11), (LEVELS, TILES), 0, TILE + 1).astype(jnp.int32)
    order = jax.random.permutation(jax.random.fold_in(key, 23), TILES)
    starts = starts.at[:, order[0]].set(0)
    starts = starts.at[:, order[1]].set(TILE)
    return starts


def draw_freq_slot(key, part):
    order = jax.random.permutation(jax.random.fold_in(key, 31), FREQS).astype(jnp.int32)
    offset = jax.random.randint(jax.random.fold_in(key, 37), (FREQS,), 0, 16).astype(jnp.int32)
    offset = jnp.where(order == 0, 0, offset)
    offset = jnp.where(order == FREQS - 1, 15, offset)
    return (order * 16 + offset).astype(jnp.int32)


def steps_of(rng, extent, shards, smallest, top_value):
    def one(position, parts):
        steps = jax.random.uniform(jax.random.fold_in(jax.random.fold_in(rng, 6), position), (parts,), jnp.float32, smallest / len(shards), top_value / len(shards))
        return jnp.repeat(jnp.exp(steps), extent[position] // parts).reshape((-1,) + (1,) * (len(extent) - position - 1))

    level = one(*shards[0])
    for cut in shards[1:]:
        level = level * one(*cut)
    return level


def bell_draw(rng, shape, spread, limit, cuts=(), dtype=jnp.bfloat16):
    entries = spread * jax.random.normal(rng, shape, jnp.float32)
    if cuts:
        entries = entries * steps_of(rng, shape, cuts, -0.22, 0.18)
    return jnp.clip(entries, -limit, limit).astype(dtype)


def setup_inputs(seed: int = 0, part: int = 0) -> dict:
    keys = jax.random.split(jax.random.key(seed), 6)
    part_keys = jax.random.split(jax.random.fold_in(keys[5], part), 6)
    return {
        "source_field": bell_draw(part_keys[0], (2, FREQS, NX, SHOTS), 1.0, 6.0, ((1, 4), (2, 4))),
        "data_field": bell_draw(part_keys[1], (2, FREQS, NX, SHOTS), 1.0, 6.0, ((1, 4), (2, 4))),
        "propagator": bell_draw(part_keys[2], (LEVELS, 2, FREQS, NX, BAND), (2 * BAND) ** -0.5, 0.125, ((2, 4), (3, 4))),
        "band_start": draw_band_start(jax.random.fold_in(jax.random.fold_in(keys[5], part), 71), part),
        "freq_slot": draw_freq_slot(jax.random.fold_in(keys[5], 71), part),
    }


def extrapolate(fields, prop_real, prop_imag, starts):
    padded = jnp.pad(fields, ((0, 0), (0, 0), (0, 0), (TILE, TILE), (0, 0)))
    pieces = []
    for tile in range(NX // TILE):
        begin = (starts[tile] + tile * TILE).astype(jnp.int32)
        window = lax.dynamic_slice_in_dim(padded, begin, BAND, 3).astype(jnp.float32)
        rows_r = prop_real[:, tile * TILE:(tile + 1) * TILE].astype(jnp.float32)
        rows_i = prop_imag[:, tile * TILE:(tile + 1) * TILE].astype(jnp.float32)
        out_r = jnp.einsum('fxb,nfbs->nfxs', rows_r, window[:, 0]) - jnp.einsum('fxb,nfbs->nfxs', rows_i, window[:, 1])
        out_i = jnp.einsum('fxb,nfbs->nfxs', rows_r, window[:, 1]) + jnp.einsum('fxb,nfbs->nfxs', rows_i, window[:, 0])
        pieces.append(jnp.stack([out_r, out_i], 1))
    return jnp.concatenate(pieces, 3).astype(jnp.bfloat16)

def reference(source_field, data_field, propagator, band_start, freq_slot):
    weight = (freq_slot.astype(jnp.float32) + 1.0) / (16.0 * FREQS)
    norm = 1.0 / math.sqrt(FREQS * SHOTS)
    source, record = (source_field, data_field)
    levels_out = []
    for level in range(LEVELS):
        both = extrapolate(jnp.stack([source, record]), propagator[level, 0], propagator[level, 1], band_start[level])
        upper, lower = (both[0], both[1])
        tiles_refl = []
        tiles_src = []
        for tile in range(NX // TILE):
            up_tile = upper[:, :, tile * TILE:(tile + 1) * TILE].astype(jnp.float32)
            down_tile = lower[:, :, tile * TILE:(tile + 1) * TILE].astype(jnp.float32)
            gram = jnp.einsum('f,cfxs,cfys->xy', weight, up_tile, down_tile) * norm
            saturated = jnp.tanh(gram).astype(jnp.bfloat16)
            scattered = jnp.einsum('xy,cfys->cfxs', saturated.astype(jnp.float32), up_tile) / math.sqrt(TILE)
            tiles_refl.append(saturated)
            tiles_src.append((up_tile + scattered).astype(jnp.bfloat16))
        levels_out.append(jnp.concatenate(tiles_refl, 0))
        source = jnp.concatenate(tiles_src, 2)
        record = lower
    return (jnp.stack(levels_out), source, record)
```

```python
import math

import jax
import jax.numpy as jnp
from jax import lax
from jax.sharding import PartitionSpec as P

LEVELS = 2


def neighbours(cells, axis):
    count = lax.axis_size(axis)
    ends = count - 1
    from_left = lax.ppermute(cells, axis, [(i, (i + 1) % count) for i in range(ends)])
    from_right = lax.ppermute(cells, axis, [((i + 1) % count, i) for i in range(ends)])
    return from_left, from_right


def advance(rows_r, rows_i, parts, start):
    extended = jnp.concatenate(parts, axis=1)
    window = lax.dynamic_slice_in_dim(extended, start, rows_r.shape[1], 1)

    def dot(a, b):
        return jnp.einsum("xb,bs->xs", a, b, preferred_element_type=jnp.float32)

    out_r = dot(rows_r, window[0]) - dot(rows_i, window[1])
    out_i = dot(rows_r, window[1]) + dot(rows_i, window[0])
    return jnp.stack([out_r, out_i]).astype(jnp.bfloat16)


def per_device(source_field, data_field, propagator, band_start, freq_slot):
    tile_len = source_field.shape[2]
    shot_count = source_field.shape[3]
    freq_total = source_field.shape[1] * lax.axis_size("freq")
    weight = (freq_slot[0].astype(jnp.float32) + 1.0) / (16.0 * freq_total)
    norm = 1.0 / math.sqrt(freq_total * shot_count)
    source, record = (source_field[:, 0], data_field[:, 0])
    record_l, record_r = neighbours(record, "lat")
    source_l, source_r = neighbours(source, "lat")
    source_parts = [source_l, source, source_r]
    levels_out = []
    for level in range(LEVELS):
        last = level == LEVELS - 1
        rows_r = propagator[level, 0, 0]
        rows_i = propagator[level, 1, 0]
        start = band_start[level, 0]
        lower = advance(rows_r, rows_i, [record_l, record, record_r], start)
        upper = advance(rows_r, rows_i, source_parts, start)
        if not last:
            record_l, record_r = neighbours(lower, "lat")
            upper_l, upper_r = neighbours(upper, "lat")
        gram = jnp.einsum("cxs,cys->xy", upper, lower, preferred_element_type=jnp.float32)
        share = lax.psum_scatter(gram * (weight * norm), "freq", scatter_dimension=0, tiled=True)
        share = jnp.tanh(share).astype(jnp.bfloat16)
        if last:
            saturated = lax.all_gather(share, "freq", axis=0, tiled=True)
            tiles, fields = ([saturated], [upper])
        else:
            share_l, share_r = neighbours(share, "lat")
            trio = lax.all_gather(jnp.stack([share_l, share, share_r]), "freq", axis=1, tiled=True)
            tiles, fields = ([trio[0], trio[1], trio[2]], [upper_l, upper, upper_r])
            saturated = trio[1]
        source_parts = [
            (
                field.astype(jnp.float32)
                + jnp.einsum("xy,cys->cxs", tile, field, preferred_element_type=jnp.float32)
                / math.sqrt(tile_len)
            ).astype(jnp.bfloat16)
            for tile, field in zip(tiles, fields)
        ]
        record = lower
        levels_out.append(saturated)
    return (jnp.stack(levels_out), source_parts[0][:, None], record[:, None])


def solution(mesh):
    return jax.shard_map(
        per_device,
        mesh=mesh,
        in_specs=(
            P("grp", "freq", "lat", None),
            P("grp", "freq", "lat", None),
            P("grp", None, "freq", "lat", None),
            P("grp", "lat"),
            P("freq"),
        ),
        out_specs=(
            P("grp", "lat", None),
            P("grp", "freq", "lat", None),
            P("grp", "freq", "lat", None),
        ),
        check_vma=False,
    )
```

```python
import functools
import math

import jax
import jax.numpy as jnp
from jax import lax
from jax.experimental import pallas as pl
from jax.experimental.pallas import tpu as pltpu
from jax.sharding import PartitionSpec as P

LEVELS = 2
F32 = jnp.float32
BF16 = jnp.bfloat16
MESH = pl.DeviceIdType.MESH
PIECES = ((1, 0), (0, 0), (1, 1), (0, 1))


def round_up(value, step):
    return (value + step - 1) // step * step


def migrate(
    lat_count,
    freq_total,
    start_ref,
    slot_ref,
    src_hbm,
    dat_hbm,
    prop_hbm,
    refl_out,
    src_out,
    dat_out,
    prop,
    rows_of,
    ext,
    scat,
    final,
    gram,
    gram_in,
    gram_x,
    refl,
    refl_flat,
    refl_wide,
    own_sem,
    prop_sem,
    out_sem,
    halo_send,
    halo_recv,
    pair_send,
    pair_recv,
    x_send,
    x_recv,
    r_send,
    r_recv,
    z_send,
    z_recv,
):
    tile = src_hbm.shape[1]
    shots = src_hbm.shape[2]
    band = prop_hbm.shape[3]
    reach = ext.shape[3]
    count_x = freq_total // 2
    half = tile // 2
    sub = half // count_x
    part = shots // 2
    lat = lax.axis_index("lat")
    freq = lax.axis_index("freq")
    core = lax.rem(freq, 2)
    chip = freq // 2
    other = 1 - core
    right = lax.rem(lat + 1, lat_count)
    left = lax.rem(lat + lat_count - 1, lat_count)
    has_right = lat < lat_count - 1
    has_left = lat > 0
    sends = (has_right, has_left)
    gets = (has_left, has_right)
    towards = (right, left)
    landing = (0, 2 * tile)
    partner = {"freq": chip * 2 + other}
    fields = (src_hbm, dat_hbm)

    def peer(step):
        return {"freq": lax.rem(chip + step, count_x) * 2 + core}

    def remote(src, dst, send, recv, device):
        return pltpu.make_async_remote_copy(
            src_ref=src, dst_ref=dst, send_sem=send, recv_sem=recv, device_id=device, device_id_type=MESH
        )

    barrier = pltpu.get_barrier_semaphore()
    greeted = [{"lat": left}, {"lat": right}, partner] + [peer(d) for d in range(1, count_x)]
    for device in greeted:
        pl.semaphore_signal(barrier, inc=1, device_id=device, device_id_type=MESH)
    pl.semaphore_wait(barrier, len(greeted))

    def halo(level, piece, way):
        field, block = PIECES[piece]
        cols = pl.ds(block * part, part)
        if level == 0:
            src = fields[field].at[:, :, cols]
        else:
            src = ext.at[1, field, :, pl.ds(tile, tile), cols]
        return remote(
            src,
            ext.at[level, field, :, pl.ds(landing[way], tile), cols],
            halo_send.at[level, piece, way],
            halo_recv.at[level, piece, way],
            {"lat": towards[way]},
        )

    def halo_start(level, piece):
        for way in range(2):
            pl.when(sends[way])(halo(level, piece, way).start)

    def halo_sent(level, piece):
        for way in range(2):
            pl.when(sends[way])(halo(level, piece, way).wait_send)

    def halo_got(level, piece):
        for way in range(2):
            pl.when(gets[way])(halo(level, piece, way).wait_recv)

    halo_start(0, 0)
    halo_start(0, 1)
    props = [pltpu.make_async_copy(prop_hbm.at[v], prop.at[v], prop_sem.at[v]) for v in range(LEVELS)]
    props[0].start()
    owns = [
        pltpu.make_async_copy(fields[f], ext.at[0, f, :, pl.ds(tile, tile)], own_sem.at[f]) for f in range(2)
    ]
    owns[1].start()
    owns[0].start()
    props[1].start()

    slack = reach - 3 * tile
    for f in range(2):
        for c in range(2):
            ext[0, f, c, pl.ds(3 * tile, slack), :] = jnp.zeros((slack, shots), BF16)
            ext[1, f, c, pl.ds(3 * tile, slack), :] = jnp.zeros((slack, shots), BF16)
    for c in range(2):
        scat[c, pl.ds(3 * tile, slack), :] = jnp.zeros((slack, shots), BF16)
    for way in range(2):

        @pl.when(jnp.logical_not(gets[way]))
        def _():
            for level in range(2):
                for f in range(2):
                    for c in range(2):
                        ext[level, f, c, pl.ds(landing[way], tile), :] = jnp.zeros((tile, shots), BF16)
            refl[2 * way] = jnp.zeros(refl.shape[1:], BF16)

    step_rows = 64

    def spread(level):
        shift = start_ref[level]

        @pl.loop(0, tile // step_rows)
        def _(i):
            rows = pl.ds(pl.multiple_of(i * step_rows, step_rows), step_rows)
            gap = jnp.zeros((step_rows, reach - band), F32)

            def moved(c):
                wide = jnp.concatenate([prop[level, c, rows, :].astype(F32), gap], axis=1)
                return pltpu.roll(wide, shift, 1)

            real = moved(0).astype(BF16)
            imag = moved(1)
            rows_of[level, 0, rows, pl.ds(0, reach)] = real
            rows_of[level, 1, rows, pl.ds(reach, reach)] = real
            rows_of[level, 1, rows, pl.ds(0, reach)] = imag.astype(BF16)
            rows_of[level, 0, rows, pl.ds(reach, reach)] = (-imag).astype(BF16)

    def advance(level, window, out, block):
        cols = pl.ds(block * part, part)

        @pl.loop(0, 2)
        def _(c):
            value = jnp.dot(
                rows_of[level, c, :, pl.ds(0, reach)], window[0, :, cols], preferred_element_type=F32
            ) + jnp.dot(
                rows_of[level, c, :, pl.ds(reach, reach)], window[1, :, cols], preferred_element_type=F32
            )
            out[c, :, cols] = value.astype(BF16)

    weight = (slot_ref[0].astype(F32) + 1.0) / (16.0 * freq_total)
    scale = weight * (1.0 / math.sqrt(freq_total * shots))
    nt = (((1,), (1,)), ((), ()))

    def gram_half(level, up, down, h):
        rows = pl.ds(pl.multiple_of(h * half, 32), half)
        value = lax.dot_general(up[0, rows, :], down[0, :, :], nt, preferred_element_type=F32)
        value += lax.dot_general(up[1, rows, :], down[1, :, :], nt, preferred_element_type=F32)
        gram[level, h] = (value * scale).reshape(count_x, sub, tile)

    def pair_copy(level):
        return remote(
            gram.at[level, other], gram_in.at[level], pair_send.at[level], pair_recv.at[level], partner
        )

    def x_copy(level, step):
        return remote(
            gram.at[level, core, lax.rem(chip + step, count_x)],
            gram_x.at[level, step - 1],
            x_send.at[level, 0, step - 1],
            x_recv.at[level, 0, step - 1],
            peer(step),
        )

    def share_copy(level, step):
        mine = refl.at[1 if level == 0 else 3, core, chip]
        return remote(mine, mine, x_send.at[level, 1, step - 1], x_recv.at[level, 1, step - 1], peer(step))

    def swap_copy(slot):
        block = refl.at[slot, core]
        return remote(block, block, r_send.at[slot], r_recv.at[slot], partner)

    def reduce(level, up, down):
        slot = 1 if level == 0 else 3
        gram_half(level, up, down, other)
        pair_copy(level).start()
        gram_half(level, up, down, core)
        pair_copy(level).wait_recv()
        for x in range(count_x):
            gram[level, core, x] = gram[level, core, x] + gram_in[level, x]
        for step in range(1, count_x):
            x_copy(level, step).start()
        total = gram[level, core, chip]
        for step in range(1, count_x):
            x_copy(level, step).wait_recv()
            total = total + gram_x[level, step - 1]
        refl[slot, core, chip] = jnp.tanh(total).astype(BF16)
        for step in range(1, count_x):
            share_copy(level, step).start()
        for step in range(1, count_x):
            share_copy(level, step).wait_recv()
        swap_copy(slot).start()

    def flatten(slot):
        for h in range(2):
            for x in range(count_x):
                rows = pl.ds(h * half + x * sub, sub)
                if sub % 16:
                    refl_wide[rows, :] = refl[slot, h, x].astype(F32)
                else:
                    refl_flat[slot, rows, :] = refl[slot, h, x]
        if sub % 16:
            refl_flat[slot] = refl_wide[...].astype(BF16)

    def z_copy(way):
        return remote(
            refl.at[1, core],
            refl.at[2 * way, core],
            z_send.at[way],
            z_recv.at[way],
            {"lat": towards[way]},
        )

    factor = 1.0 / math.sqrt(tile)

    def scatter(block):
        cols = pl.ds(block * part, part)

        @pl.loop(0, 6)
        def _(i):
            c = i // 3
            place = lax.rem(i, 3)
            rows = pl.ds(pl.multiple_of(place * tile, 64), tile)
            up = ext[1, 0, c, rows, cols]
            add = jnp.dot(refl_flat[place], up, preferred_element_type=F32)
            scat[c, rows, cols] = (up.astype(F32) + add * factor).astype(BF16)

    own = pl.ds(tile, tile)
    props[0].wait()
    spread(0)
    props[1].wait()
    spread(1)
    for copy in owns:
        copy.wait()
    for piece, (field, block) in enumerate(PIECES):
        halo_got(0, piece)
        if piece + 2 < 4:
            halo_sent(0, piece)
            halo_start(0, piece + 2)
        else:
            halo_start(1, piece - 2)
        advance(0, ext.at[0, field], ext.at[1, field, :, own], block)
    halo_start(1, 2)
    halo_start(1, 3)
    reduce(0, ext.at[1, 0, :, own], ext.at[1, 1, :, own])
    for way in range(2):
        pl.when(sends[way])(z_copy(way).start)
    swap_copy(1).wait_recv()
    flatten(1)
    refl_store = pltpu.make_async_copy(refl_flat.at[1], refl_out.at[0], out_sem.at[0])
    refl_store.start()
    halo_got(1, 0)
    advance(1, ext.at[1, 1], final.at[1], 0)
    for way in range(2):

        @pl.when(gets[way])
        def _():
            z_copy(way).wait_recv()
            swap_copy(2 * way).start()

    for way in range(2):

        pl.when(gets[way])(swap_copy(2 * way).wait_recv)
        flatten(2 * way)
    halo_got(1, 1)
    scatter(0)
    advance(1, scat, final.at[0], 0)
    halo_got(1, 2)
    advance(1, ext.at[1, 1], final.at[1], 1)
    dat_store = pltpu.make_async_copy(final.at[1], dat_out, out_sem.at[1])
    dat_store.start()
    halo_got(1, 3)
    scatter(1)
    advance(1, scat, final.at[0], 1)
    reduce(1, final.at[0], final.at[1])
    swap_copy(3).wait_recv()
    flatten(3)
    refl_last = pltpu.make_async_copy(refl_flat.at[3], refl_out.at[1], out_sem.at[2])
    refl_last.start()

    @pl.loop(0, 2)
    def _(c):
        up = final[0, c]
        add = jnp.dot(refl_flat[3], up, preferred_element_type=F32)
        scat[c, pl.ds(0, tile), :] = (up.astype(F32) + add * factor).astype(BF16)

    src_store = pltpu.make_async_copy(scat.at[:, pl.ds(0, tile)], src_out, out_sem.at[3])
    src_store.start()
    for piece in range(4):
        if piece >= 2:
            halo_sent(0, piece)
        halo_sent(1, piece)
    for way in range(2):
        pl.when(sends[way])(z_copy(way).wait_send)
        pl.when(gets[way])(swap_copy(2 * way).wait_send)
    swap_copy(1).wait_send()
    swap_copy(3).wait_send()
    for level in range(2):
        pair_copy(level).wait_send()
        for step in range(1, count_x):
            x_copy(level, step).wait_send()
            share_copy(level, step).wait_send()
    for store in (refl_store, dat_store, refl_last, src_store):
        store.wait()


def per_device(source_field, data_field, propagator, band_start, freq_slot):
    tile = source_field.shape[2]
    shots = source_field.shape[3]
    band = propagator.shape[4]
    lat_count = lax.axis_size("lat")
    freq_total = source_field.shape[1] * lax.axis_size("freq")
    count_x = freq_total // 2
    sub = tile // 2 // count_x
    reach = round_up(3 * tile, 256)
    vmem = pltpu.VMEM
    dma = pltpu.SemaphoreType.DMA
    field = jax.ShapeDtypeStruct((2, tile, shots), BF16)
    refl, src, dat = pl.pallas_call(
        functools.partial(migrate, lat_count, freq_total),
        out_shape=(jax.ShapeDtypeStruct((LEVELS, tile, tile), BF16), field, field),
        in_specs=[pl.BlockSpec(memory_space=pltpu.SMEM)] * 2 + [pl.BlockSpec(memory_space=pl.ANY)] * 3,
        out_specs=[pl.BlockSpec(memory_space=pl.ANY)] * 3,
        scratch_shapes=[
            vmem((LEVELS, 2, tile, band), BF16),
            vmem((LEVELS, 2, tile, 2 * reach), BF16),
            vmem((LEVELS, 2, 2, reach, shots), BF16),
            vmem((2, reach, shots), BF16),
            vmem((2, 2, tile, shots), BF16),
            vmem((LEVELS, 2, count_x, sub, tile), F32),
            vmem((LEVELS, count_x, sub, tile), F32),
            vmem((LEVELS, count_x - 1, sub, tile), F32),
            vmem((4, 2, count_x, sub, tile), BF16),
            vmem((4, tile, tile), BF16),
            vmem((tile if sub % 16 else 8, tile), F32),
            dma((2,)),
            dma((2,)),
            dma((4,)),
            dma((LEVELS, 4, 2)),
            dma((LEVELS, 4, 2)),
            dma((LEVELS,)),
            dma((LEVELS,)),
            dma((LEVELS, 2, count_x - 1)),
            dma((LEVELS, 2, count_x - 1)),
            dma((4,)),
            dma((4,)),
            dma((2,)),
            dma((2,)),
        ],
        compiler_params=pltpu.CompilerParams(
            collective_id=0, has_side_effects=True, vmem_limit_bytes=60 * 1024 * 1024
        ),
    )(
        band_start[:, 0],
        freq_slot,
        source_field[:, 0],
        data_field[:, 0],
        propagator[:, :, 0],
    )
    return refl, src[:, None], dat[:, None]


def solution(mesh):
    return jax.shard_map(
        per_device,
        mesh=mesh,
        in_specs=(
            P("grp", "freq", "lat", None),
            P("grp", "freq", "lat", None),
            P("grp", None, "freq", "lat", None),
            P("grp", "lat"),
            P("freq"),
        ),
        out_specs=(
            P("grp", "lat", None),
            P("grp", "freq", "lat", None),
            P("grp", "freq", "lat", None),
        ),
        check_vma=False,
    )
```

```python
import functools
import math

import jax
import jax.numpy as jnp
from jax import lax
from jax.experimental import pallas as pl
from jax.experimental.pallas import tpu as pltpu
from jax.sharding import PartitionSpec as P

LEVELS = 2
F32 = jnp.float32
BF16 = jnp.bfloat16
MESH = pl.DeviceIdType.MESH
PIECES = ((1, 0), (0, 0), (0, 1), (1, 1))


def round_up(value, step):
    return (value + step - 1) // step * step


def migrate(
    lat_count,
    freq_total,
    start_ref,
    slot_ref,
    src_hbm,
    dat_hbm,
    prop_hbm,
    refl_out,
    src_out,
    dat_out,
    prop,
    rows_of,
    ext,
    scat,
    final,
    gram,
    gram_in,
    gram_out,
    gram_x,
    refl,
    refl_flat,
    refl_wide,
    own_sem,
    prop_sem,
    out_sem,
    halo_send,
    halo_recv,
    pair_send,
    pair_recv,
    x_send,
    x_recv,
    share_send,
    share_recv,
    swap_send,
    swap_recv,
    z_send,
    z_recv,
):
    tile = src_hbm.shape[1]
    shots = src_hbm.shape[2]
    band = prop_hbm.shape[3]
    reach = ext.shape[3]
    count_x = freq_total // 2
    half = tile // 2
    sub = half // count_x
    part = shots // 2
    lat = lax.axis_index("lat")
    freq = lax.axis_index("freq")
    core = lax.rem(freq, 2)
    chip = freq // 2
    other = 1 - core
    right = lax.rem(lat + 1, lat_count)
    left = lax.rem(lat + lat_count - 1, lat_count)
    has_right = lat < lat_count - 1
    has_left = lat > 0
    sends = (has_right, has_left)
    gets = (has_left, has_right)
    towards = (right, left)
    landing = (0, 2 * tile)
    partner = {"freq": chip * 2 + other}
    fields = (src_hbm, dat_hbm)

    def peer(step):
        return {"freq": lax.rem(chip + step, count_x) * 2 + core}

    def remote(src, dst, send, recv, device):
        return pltpu.make_async_remote_copy(
            src_ref=src, dst_ref=dst, send_sem=send, recv_sem=recv, device_id=device, device_id_type=MESH
        )

    barrier = pltpu.get_barrier_semaphore()
    greeted = [{"lat": left}, {"lat": right}, partner] + [peer(d) for d in range(1, count_x)]
    for device in greeted:
        pl.semaphore_signal(barrier, inc=1, device_id=device, device_id_type=MESH)
    pl.semaphore_wait(barrier, len(greeted))

    def halo(level, piece, way):
        field, block = PIECES[piece]
        cols = pl.ds(block * part, part)
        if level == 0:
            src = fields[field].at[:, :, cols]
        else:
            src = ext.at[1, field, :, pl.ds(tile, tile), cols]
        return remote(
            src,
            ext.at[level, field, :, pl.ds(landing[way], tile), cols],
            halo_send.at[level, piece, way],
            halo_recv.at[level, piece, way],
            {"lat": towards[way]},
        )

    def halo_start(level, piece):
        for way in range(2):
            pl.when(sends[way])(halo(level, piece, way).start)

    def halo_sent(level, piece):
        for way in range(2):
            pl.when(sends[way])(halo(level, piece, way).wait_send)

    def halo_got(level, piece):
        for way in range(2):
            pl.when(gets[way])(halo(level, piece, way).wait_recv)

    halo_start(0, 0)
    halo_start(0, 1)
    props = [pltpu.make_async_copy(prop_hbm.at[v], prop.at[v], prop_sem.at[v]) for v in range(LEVELS)]
    props[0].start()
    owns = [
        pltpu.make_async_copy(fields[f], ext.at[0, f, :, pl.ds(tile, tile)], own_sem.at[f]) for f in range(2)
    ]
    owns[1].start()
    owns[0].start()
    props[1].start()

    slack = reach - 3 * tile
    for f in range(2):
        for c in range(2):
            ext[0, f, c, pl.ds(3 * tile, slack), :] = jnp.zeros((slack, shots), BF16)
            ext[1, f, c, pl.ds(3 * tile, slack), :] = jnp.zeros((slack, shots), BF16)
    for c in range(2):
        scat[c, pl.ds(3 * tile, slack), :] = jnp.zeros((slack, shots), BF16)
    for way in range(2):

        @pl.when(jnp.logical_not(gets[way]))
        def _():
            for level in range(2):
                for f in range(2):
                    for c in range(2):
                        ext[level, f, c, pl.ds(landing[way], tile), :] = jnp.zeros((tile, shots), BF16)
            refl[2 * way] = jnp.zeros(refl.shape[1:], BF16)

    step_rows = 64

    def spread(level):
        shift = start_ref[level]

        @pl.loop(0, tile // step_rows)
        def _(i):
            rows = pl.ds(pl.multiple_of(i * step_rows, step_rows), step_rows)
            gap = jnp.zeros((step_rows, reach - band), F32)

            def moved(c):
                wide = jnp.concatenate([prop[level, c, rows, :].astype(F32), gap], axis=1)
                return pltpu.roll(wide, shift, 1)

            real = moved(0).astype(BF16)
            imag = moved(1)
            rows_of[level, 0, rows, pl.ds(0, reach)] = real
            rows_of[level, 1, rows, pl.ds(reach, reach)] = real
            rows_of[level, 1, rows, pl.ds(0, reach)] = imag.astype(BF16)
            rows_of[level, 0, rows, pl.ds(reach, reach)] = (-imag).astype(BF16)

    def advance(level, window, out, block):
        cols = pl.ds(block * part, part)

        @pl.loop(0, 2)
        def _(c):
            value = jnp.dot(
                rows_of[level, c, :, pl.ds(0, reach)], window[0, :, cols], preferred_element_type=F32
            ) + jnp.dot(
                rows_of[level, c, :, pl.ds(reach, reach)], window[1, :, cols], preferred_element_type=F32
            )
            out[c, :, cols] = value.astype(BF16)

    weight = (slot_ref[0].astype(F32) + 1.0) / (16.0 * freq_total)
    scale = weight * (1.0 / math.sqrt(freq_total * shots))
    nt = (((1,), (1,)), ((), ()))

    def gram_half(level, up, down, h, block):
        rows = pl.ds(pl.multiple_of(h * half, 32), half)
        cols = pl.ds(block * part, part)
        value = lax.dot_general(up[0, rows, cols], down[0, :, cols], nt, preferred_element_type=F32)
        value += lax.dot_general(up[1, rows, cols], down[1, :, cols], nt, preferred_element_type=F32)
        value = (value * scale).reshape(count_x, sub, tile)
        if block:
            value = value + gram[level, h]
        gram[level, h] = value

    def ahead(step):
        return lax.rem(chip + step, count_x)

    def behind(step):
        return lax.rem(chip + count_x - step, count_x)

    def pair_copy(level, step):
        return remote(
            gram.at[level, other, ahead(step)],
            gram_in.at[level, ahead(step)],
            pair_send.at[level, step],
            pair_recv.at[level, step],
            partner,
        )

    def x_copy(level, step):
        return remote(
            gram_out.at[level, step - 1],
            gram_x.at[level, step - 1],
            x_send.at[level, step - 1],
            x_recv.at[level, step - 1],
            peer(step),
        )

    def share_copy(slot, step):
        mine = refl.at[slot, core, chip]
        return remote(mine, mine, share_send.at[slot, step - 1], share_recv.at[slot, step - 1], peer(step))

    def swap_copy(slot, step):
        block = refl.at[slot, core, behind(step)]
        return remote(block, block, swap_send.at[slot, step], swap_recv.at[slot, step], partner)

    def share_start(slot):
        for step in range(1, count_x):
            share_copy(slot, step).start()
        swap_copy(slot, 0).start()

    def share_finish(slot):
        for step in range(1, count_x):
            share_copy(slot, step).wait_recv()
            swap_copy(slot, step).start()
        for step in range(count_x):
            swap_copy(slot, step).wait_recv()

    def share_sent(slot):
        for step in range(1, count_x):
            share_copy(slot, step).wait_send()
        for step in range(count_x):
            swap_copy(slot, step).wait_send()

    def reduce(level, slot, up, down):
        order = list(range(1, count_x)) + [0]
        gram_half(level, up, down, other, 1)
        for step in order:
            pair_copy(level, step).start()
        gram_half(level, up, down, core, 1)
        for step in order:
            pair_copy(level, step).wait_recv()
            total = gram[level, core, ahead(step)] + gram_in[level, ahead(step)]
            if step:
                gram_out[level, step - 1] = total.astype(BF16)
                x_copy(level, step).start()
        for step in range(1, count_x):
            x_copy(level, step).wait_recv()
            total = total + gram_x[level, step - 1].astype(F32)
        refl[slot, core, chip] = jnp.tanh(total).astype(BF16)

    def flatten(slot):
        for h in range(2):
            for x in range(count_x):
                rows = pl.ds(h * half + x * sub, sub)
                if sub % 16:
                    refl_wide[rows, :] = refl[slot, h, x].astype(F32)
                else:
                    refl_flat[slot, rows, :] = refl[slot, h, x]
        if sub % 16:
            refl_flat[slot] = refl_wide[...].astype(BF16)

    def z_copy(way):
        return remote(
            refl.at[1, core, chip],
            refl.at[2 * way, core, chip],
            z_send.at[way],
            z_recv.at[way],
            {"lat": towards[way]},
        )

    factor = 1.0 / math.sqrt(tile)

    def scatter(block):
        cols = pl.ds(block * part, part)

        @pl.loop(0, 6)
        def _(i):
            c = i // 3
            place = lax.rem(i, 3)
            rows = pl.ds(pl.multiple_of(place * tile, 64), tile)
            up = ext[1, 0, c, rows, cols]
            add = jnp.dot(refl_flat[place], up, preferred_element_type=F32)
            scat[c, rows, cols] = (up.astype(F32) + add * factor).astype(BF16)

    own = pl.ds(tile, tile)
    props[0].wait()
    spread(0)
    props[1].wait()
    spread(1)
    for copy in owns:
        copy.wait()
    for piece, (field, block) in enumerate(PIECES):
        halo_got(0, piece)
        if piece + 2 < 4:
            halo_sent(0, piece)
            halo_start(0, piece + 2)
        else:
            halo_start(1, piece - 2)
        advance(0, ext.at[0, field], ext.at[1, field, :, own], block)
        if piece == 1:
            for h in range(2):
                gram_half(0, ext.at[1, 0, :, own], ext.at[1, 1, :, own], h, 0)
    halo_start(1, 2)
    reduce(0, 1, ext.at[1, 0, :, own], ext.at[1, 1, :, own])
    for way in range(2):
        pl.when(sends[way])(z_copy(way).start)
    share_start(1)
    halo_start(1, 3)
    share_finish(1)
    flatten(1)
    refl_store = pltpu.make_async_copy(refl_flat.at[1], refl_out.at[0], out_sem.at[0])
    refl_store.start()
    for way in range(2):

        @pl.when(gets[way])
        def _():
            z_copy(way).wait_recv()
            share_start(2 * way)

    halo_got(1, 0)
    advance(1, ext.at[1, 1], final.at[1], 0)
    for way in range(2):
        pl.when(gets[way])(functools.partial(share_finish, 2 * way))
        flatten(2 * way)
    halo_got(1, 1)
    scatter(0)
    advance(1, scat, final.at[0], 0)
    for h in range(2):
        gram_half(1, final.at[0], final.at[1], h, 0)
    halo_got(1, 2)
    scatter(1)
    advance(1, scat, final.at[0], 1)
    src_store = pltpu.make_async_copy(final.at[0], src_out, out_sem.at[3])
    src_store.start()
    halo_got(1, 3)
    advance(1, ext.at[1, 1], final.at[1], 1)
    dat_store = pltpu.make_async_copy(final.at[1], dat_out, out_sem.at[1])
    reduce(1, 3, final.at[0], final.at[1])
    share_start(3)
    dat_store.start()
    share_finish(3)
    flatten(3)
    refl_last = pltpu.make_async_copy(refl_flat.at[3], refl_out.at[1], out_sem.at[2])
    refl_last.start()
    for piece in range(4):
        if piece >= 2:
            halo_sent(0, piece)
        halo_sent(1, piece)
    for way in range(2):
        pl.when(sends[way])(z_copy(way).wait_send)
        pl.when(gets[way])(functools.partial(share_sent, 2 * way))
    share_sent(1)
    share_sent(3)
    for level in range(2):
        for step in range(count_x):
            pair_copy(level, step).wait_send()
        for step in range(1, count_x):
            x_copy(level, step).wait_send()
    for store in (refl_store, dat_store, refl_last, src_store):
        store.wait()


def finish(refl_in, up_in, dat_in, refl_out, src_out, dat_out, refl, up, dat, done, in_sem, out_sem):
    tile = up_in.shape[1]
    factor = 1.0 / math.sqrt(tile)
    last = LEVELS - 1
    moves = [(refl_in.at[v], refl.at[v], refl_out.at[v]) for v in range(last, -1, -1)]
    moves += [(dat_in.at[c], dat.at[c], dat_out.at[c]) for c in range(2)]
    fetch = [pltpu.make_async_copy(up_in.at[c], up.at[c], in_sem.at[c]) for c in range(2)]
    loads = [pltpu.make_async_copy(m[0], m[1], in_sem.at[2 + i]) for i, m in enumerate(moves)]
    stores = [pltpu.make_async_copy(m[1], m[2], out_sem.at[2 + i]) for i, m in enumerate(moves)]
    for load in [loads[0]] + fetch + loads[1:]:
        load.start()
    loads[0].wait()
    stores[0].start()
    for c in range(2):
        fetch[c].wait()
        field = up[c]
        add = jnp.dot(refl[last], field, preferred_element_type=F32)
        done[c] = (field.astype(F32) + add * factor).astype(BF16)
        store = pltpu.make_async_copy(done.at[c], src_out.at[c], out_sem.at[c])
        store.start()
        stores.append(store)
        for i in range(1 + c, len(moves), 2):
            loads[i].wait()
            stores[i].start()
    for store in stores:
        store.wait()


def per_device(source_field, data_field, propagator, band_start, freq_slot):
    tile = source_field.shape[2]
    shots = source_field.shape[3]
    band = propagator.shape[4]
    lat_count = lax.axis_size("lat")
    freq_total = source_field.shape[1] * lax.axis_size("freq")
    count_x = freq_total // 2
    sub = tile // 2 // count_x
    reach = round_up(3 * tile, 256)
    vmem = pltpu.VMEM
    dma = pltpu.SemaphoreType.DMA
    field = jax.ShapeDtypeStruct((2, tile, shots), BF16)
    whole = jax.ShapeDtypeStruct((LEVELS, tile, tile), BF16)
    refl, up, dat = pl.pallas_call(
        functools.partial(migrate, lat_count, freq_total),
        out_shape=(whole, field, field),
        in_specs=[pl.BlockSpec(memory_space=pltpu.SMEM)] * 2 + [pl.BlockSpec(memory_space=pl.ANY)] * 3,
        out_specs=[pl.BlockSpec(memory_space=pl.ANY)] * 3,
        scratch_shapes=[
            vmem((LEVELS, 2, tile, band), BF16),
            vmem((LEVELS, 2, tile, 2 * reach), BF16),
            vmem((LEVELS, 2, 2, reach, shots), BF16),
            vmem((2, reach, shots), BF16),
            vmem((2, 2, tile, shots), BF16),
            vmem((LEVELS, 2, count_x, sub, tile), F32),
            vmem((LEVELS, count_x, sub, tile), F32),
            vmem((LEVELS, count_x - 1, sub, tile), BF16),
            vmem((LEVELS, count_x - 1, sub, tile), BF16),
            vmem((4, 2, count_x, sub, tile), BF16),
            vmem((4, tile, tile), BF16),
            vmem((tile if sub % 16 else 8, tile), F32),
            dma((2,)),
            dma((2,)),
            dma((4,)),
            dma((LEVELS, 4, 2)),
            dma((LEVELS, 4, 2)),
            dma((LEVELS, count_x)),
            dma((LEVELS, count_x)),
            dma((LEVELS, count_x - 1)),
            dma((LEVELS, count_x - 1)),
            dma((4, count_x - 1)),
            dma((4, count_x - 1)),
            dma((4, count_x)),
            dma((4, count_x)),
            dma((2,)),
            dma((2,)),
        ],
        compiler_params=pltpu.CompilerParams(
            collective_id=0, has_side_effects=True, vmem_limit_bytes=60 * 1024 * 1024
        ),
    )(
        band_start[:, 0],
        freq_slot,
        source_field[:, 0],
        data_field[:, 0],
        propagator[:, :, 0],
    )
    refl, src, dat = pl.pallas_call(
        finish,
        out_shape=(whole, field, field),
        in_specs=[pl.BlockSpec(memory_space=pl.ANY)] * 3,
        out_specs=[pl.BlockSpec(memory_space=pl.ANY)] * 3,
        scratch_shapes=[
            vmem((LEVELS, tile, tile), BF16),
            vmem((2, tile, shots), BF16),
            vmem((2, tile, shots), BF16),
            vmem((2, tile, shots), BF16),
            dma((4 + LEVELS,)),
            dma((4 + LEVELS,)),
        ],
    )(refl, up, dat)
    return refl, src[:, None], dat[:, None]


def solution(mesh):
    return jax.shard_map(
        per_device,
        mesh=mesh,
        in_specs=(
            P("grp", "freq", "lat", None),
            P("grp", "freq", "lat", None),
            P("grp", None, "freq", "lat", None),
            P("grp", "lat"),
            P("freq"),
        ),
        out_specs=(
            P("grp", "lat", None),
            P("grp", "freq", "lat", None),
            P("grp", "freq", "lat", None),
        ),
        check_vma=False,
    )
```

```python
import functools
import math

import jax
import jax.numpy as jnp
from jax import lax
from jax.experimental import pallas as pl
from jax.experimental.pallas import tpu as pltpu
from jax.sharding import PartitionSpec as P

LEVELS = 2
F32 = jnp.float32
BF16 = jnp.bfloat16
MESH = pl.DeviceIdType.MESH
PIECES = ((1, 0), (0, 0), (0, 1), (1, 1))


def round_up(value, step):
    return (value + step - 1) // step * step


def migrate(
    lat_count,
    freq_total,
    start_ref,
    slot_ref,
    src_hbm,
    dat_hbm,
    prop_hbm,
    refl_out,
    src_out,
    dat_out,
    prop,
    rows_of,
    ext,
    scat,
    final,
    gram,
    gram_in,
    gram_out,
    gram_x,
    refl,
    refl_flat,
    refl_wide,
    own_sem,
    prop_sem,
    out_sem,
    halo_send,
    halo_recv,
    pair_send,
    pair_recv,
    x_send,
    x_recv,
    share_send,
    share_recv,
    swap_send,
    swap_recv,
    z_send,
    z_recv,
):
    tile = src_hbm.shape[1]
    shots = src_hbm.shape[2]
    band = prop_hbm.shape[3]
    reach = ext.shape[3]
    count_x = freq_total // 2
    half = tile // 2
    sub = half // count_x
    part = shots // 2
    lat = lax.axis_index("lat")
    freq = lax.axis_index("freq")
    core = lax.rem(freq, 2)
    chip = freq // 2
    other = 1 - core
    right = lax.rem(lat + 1, lat_count)
    left = lax.rem(lat + lat_count - 1, lat_count)
    has_right = lat < lat_count - 1
    has_left = lat > 0
    sends = (has_right, has_left)
    gets = (has_left, has_right)
    towards = (right, left)
    landing = (0, 2 * tile)
    partner = {"freq": chip * 2 + other}
    fields = (src_hbm, dat_hbm)

    def peer(step):
        return {"freq": lax.rem(chip + step, count_x) * 2 + core}

    def remote(src, dst, send, recv, device):
        return pltpu.make_async_remote_copy(
            src_ref=src, dst_ref=dst, send_sem=send, recv_sem=recv, device_id=device, device_id_type=MESH
        )

    barrier = pltpu.get_barrier_semaphore()
    greeted = [{"lat": left}, {"lat": right}, partner] + [peer(d) for d in range(1, count_x)]
    for device in greeted:
        pl.semaphore_signal(barrier, inc=1, device_id=device, device_id_type=MESH)
    pl.semaphore_wait(barrier, len(greeted))

    def halo(level, piece, way):
        field, block = PIECES[piece]
        cols = pl.ds(block * part, part)
        if level == 0:
            src = fields[field].at[:, :, cols]
        else:
            src = ext.at[1, field, :, pl.ds(tile, tile), cols]
        return remote(
            src,
            ext.at[level, field, :, pl.ds(landing[way], tile), cols],
            halo_send.at[level, piece, way],
            halo_recv.at[level, piece, way],
            {"lat": towards[way]},
        )

    def halo_start(level, piece):
        for way in range(2):
            pl.when(sends[way])(halo(level, piece, way).start)

    def halo_sent(level, piece):
        for way in range(2):
            pl.when(sends[way])(halo(level, piece, way).wait_send)

    def halo_got(level, piece):
        for way in range(2):
            pl.when(gets[way])(halo(level, piece, way).wait_recv)

    halo_start(0, 0)
    halo_start(0, 1)
    props = [pltpu.make_async_copy(prop_hbm.at[v], prop.at[v], prop_sem.at[v]) for v in range(LEVELS)]
    props[0].start()
    owns = [
        pltpu.make_async_copy(fields[f], ext.at[0, f, :, pl.ds(tile, tile)], own_sem.at[f]) for f in range(2)
    ]
    owns[1].start()
    owns[0].start()
    props[1].start()

    slack = reach - 3 * tile
    for f in range(2):
        for c in range(2):
            ext[0, f, c, pl.ds(3 * tile, slack), :] = jnp.zeros((slack, shots), BF16)
            ext[1, f, c, pl.ds(3 * tile, slack), :] = jnp.zeros((slack, shots), BF16)
    for c in range(2):
        scat[c, pl.ds(3 * tile, slack), :] = jnp.zeros((slack, shots), BF16)
    for way in range(2):

        @pl.when(jnp.logical_not(gets[way]))
        def _():
            for level in range(2):
                for f in range(2):
                    for c in range(2):
                        ext[level, f, c, pl.ds(landing[way], tile), :] = jnp.zeros((tile, shots), BF16)
            refl[2 * way] = jnp.zeros(refl.shape[1:], BF16)

    step_rows = 64

    def spread(level):
        shift = start_ref[level]

        @pl.loop(0, tile // step_rows)
        def _(i):
            rows = pl.ds(pl.multiple_of(i * step_rows, step_rows), step_rows)
            gap = jnp.zeros((step_rows, reach - band), F32)

            def moved(c):
                wide = jnp.concatenate([prop[level, c, rows, :].astype(F32), gap], axis=1)
                return pltpu.roll(wide, shift, 1)

            real = moved(0).astype(BF16)
            imag = moved(1)
            rows_of[level, 0, rows, pl.ds(0, reach)] = real
            rows_of[level, 1, rows, pl.ds(reach, reach)] = real
            rows_of[level, 1, rows, pl.ds(0, reach)] = imag.astype(BF16)
            rows_of[level, 0, rows, pl.ds(reach, reach)] = (-imag).astype(BF16)

    def advance(level, window, out, block):
        cols = pl.ds(block * part, part)

        @pl.loop(0, 2)
        def _(c):
            value = jnp.dot(
                rows_of[level, c, :, pl.ds(0, reach)], window[0, :, cols], preferred_element_type=F32
            ) + jnp.dot(
                rows_of[level, c, :, pl.ds(reach, reach)], window[1, :, cols], preferred_element_type=F32
            )
            out[c, :, cols] = value.astype(BF16)

    weight = (slot_ref[0].astype(F32) + 1.0) / (16.0 * freq_total)
    scale = weight * (1.0 / math.sqrt(freq_total * shots))
    nt = (((1,), (1,)), ((), ()))

    def gram_half(level, up, down, h, block):
        rows = pl.ds(pl.multiple_of(h * half, 32), half)
        cols = pl.ds(block * part, part)
        value = lax.dot_general(up[0, rows, cols], down[0, :, cols], nt, preferred_element_type=F32)
        value += lax.dot_general(up[1, rows, cols], down[1, :, cols], nt, preferred_element_type=F32)
        value = (value * scale).reshape(count_x, sub, tile)
        if block:
            value = value + gram[level, h]
        gram[level, h] = value

    def ahead(step):
        return lax.rem(chip + step, count_x)

    def behind(step):
        return lax.rem(chip + count_x - step, count_x)

    def pair_copy(level, step):
        return remote(
            gram.at[level, other, ahead(step)],
            gram_in.at[level, ahead(step)],
            pair_send.at[level, step],
            pair_recv.at[level, step],
            partner,
        )

    def x_copy(level, step):
        return remote(
            gram_out.at[level, step - 1],
            gram_x.at[level, step - 1],
            x_send.at[level, step - 1],
            x_recv.at[level, step - 1],
            peer(step),
        )

    def share_copy(slot, step):
        mine = refl.at[slot, core, chip]
        return remote(mine, mine, share_send.at[slot, step - 1], share_recv.at[slot, step - 1], peer(step))

    def swap_copy(slot, step):
        block = refl.at[slot, core, behind(step)]
        return remote(block, block, swap_send.at[slot, step], swap_recv.at[slot, step], partner)

    def share_start(slot):
        for step in range(1, count_x):
            share_copy(slot, step).start()
        swap_copy(slot, 0).start()

    def share_finish(slot):
        for step in range(1, count_x):
            share_copy(slot, step).wait_recv()
            swap_copy(slot, step).start()
        for step in range(count_x):
            swap_copy(slot, step).wait_recv()

    def share_sent(slot):
        for step in range(1, count_x):
            share_copy(slot, step).wait_send()
        for step in range(count_x):
            swap_copy(slot, step).wait_send()

    def reduce(level, slot, up, down):
        order = list(range(1, count_x)) + [0]
        gram_half(level, up, down, other, 1)
        for step in order:
            pair_copy(level, step).start()
        gram_half(level, up, down, core, 1)
        for step in order:
            pair_copy(level, step).wait_recv()
            total = gram[level, core, ahead(step)] + gram_in[level, ahead(step)]
            if step:
                gram_out[level, step - 1] = total.astype(BF16)
                x_copy(level, step).start()
        for step in range(1, count_x):
            x_copy(level, step).wait_recv()
            total = total + gram_x[level, step - 1].astype(F32)
        refl[slot, core, chip] = jnp.tanh(total).astype(BF16)

    def flatten(slot):
        for h in range(2):
            for x in range(count_x):
                rows = pl.ds(h * half + x * sub, sub)
                if sub % 16:
                    refl_wide[rows, :] = refl[slot, h, x].astype(F32)
                else:
                    refl_flat[slot, rows, :] = refl[slot, h, x]
        if sub % 16:
            refl_flat[slot] = refl_wide[...].astype(BF16)

    def z_copy(way):
        return remote(
            refl.at[1, core, chip],
            refl.at[2 * way, core, chip],
            z_send.at[way],
            z_recv.at[way],
            {"lat": towards[way]},
        )

    factor = 1.0 / math.sqrt(tile)

    def scatter(block):
        cols = pl.ds(block * part, part)

        @pl.loop(0, 6)
        def _(i):
            c = i // 3
            place = lax.rem(i, 3)
            rows = pl.ds(pl.multiple_of(place * tile, 64), tile)
            up = ext[1, 0, c, rows, cols]
            add = jnp.dot(refl_flat[place], up, preferred_element_type=F32)
            scat[c, rows, cols] = (up.astype(F32) + add * factor).astype(BF16)

    own = pl.ds(tile, tile)
    props[0].wait()
    spread(0)
    props[1].wait()
    spread(1)
    for copy in owns:
        copy.wait()
    for piece, (field, block) in enumerate(PIECES):
        halo_got(0, piece)
        if piece + 2 < 4:
            halo_sent(0, piece)
            halo_start(0, piece + 2)
        else:
            halo_start(1, piece - 2)
        advance(0, ext.at[0, field], ext.at[1, field, :, own], block)
        if piece == 1:
            for h in range(2):
                gram_half(0, ext.at[1, 0, :, own], ext.at[1, 1, :, own], h, 0)
    reduce(0, 1, ext.at[1, 0, :, own], ext.at[1, 1, :, own])
    for way in range(2):
        pl.when(sends[way])(z_copy(way).start)
    share_start(1)
    halo_start(1, 2)
    halo_start(1, 3)
    share_finish(1)
    flatten(1)
    refl_store = pltpu.make_async_copy(refl_flat.at[1], refl_out.at[0], out_sem.at[0])
    refl_store.start()
    for way in range(2):

        @pl.when(gets[way])
        def _():
            z_copy(way).wait_recv()
            share_start(2 * way)

    halo_got(1, 0)
    advance(1, ext.at[1, 1], final.at[1], 0)
    for way in range(2):
        pl.when(gets[way])(functools.partial(share_finish, 2 * way))
        flatten(2 * way)
    halo_got(1, 1)
    scatter(0)
    advance(1, scat, final.at[0], 0)
    for h in range(2):
        gram_half(1, final.at[0], final.at[1], h, 0)
    halo_got(1, 2)
    scatter(1)
    advance(1, scat, final.at[0], 1)
    src_store = pltpu.make_async_copy(final.at[0], src_out, out_sem.at[3])
    src_store.start()
    halo_got(1, 3)
    advance(1, ext.at[1, 1], final.at[1], 1)
    dat_store = pltpu.make_async_copy(final.at[1], dat_out, out_sem.at[1])
    reduce(1, 3, final.at[0], final.at[1])
    share_start(3)
    dat_store.start()
    share_finish(3)
    flatten(3)
    refl_last = pltpu.make_async_copy(refl_flat.at[3], refl_out.at[1], out_sem.at[2])
    refl_last.start()
    for piece in range(4):
        if piece >= 2:
            halo_sent(0, piece)
        halo_sent(1, piece)
    for way in range(2):
        pl.when(sends[way])(z_copy(way).wait_send)
        pl.when(gets[way])(functools.partial(share_sent, 2 * way))
    share_sent(1)
    share_sent(3)
    for level in range(2):
        for step in range(count_x):
            pair_copy(level, step).wait_send()
        for step in range(1, count_x):
            x_copy(level, step).wait_send()
    for store in (refl_store, dat_store, refl_last, src_store):
        store.wait()


def finish(refl_in, up_in, dat_in, refl_out, src_out, dat_out, refl, up, dat, done, in_sem, out_sem):
    tile = up_in.shape[1]
    factor = 1.0 / math.sqrt(tile)
    last = LEVELS - 1
    moves = [(refl_in.at[v], refl.at[v], refl_out.at[v]) for v in range(last, -1, -1)]
    moves += [(dat_in.at[c], dat.at[c], dat_out.at[c]) for c in range(2)]
    fetch = [pltpu.make_async_copy(up_in.at[c], up.at[c], in_sem.at[c]) for c in range(2)]
    loads = [pltpu.make_async_copy(m[0], m[1], in_sem.at[2 + i]) for i, m in enumerate(moves)]
    stores = [pltpu.make_async_copy(m[1], m[2], out_sem.at[2 + i]) for i, m in enumerate(moves)]
    for load in [loads[0]] + fetch + loads[1:]:
        load.start()
    loads[0].wait()
    stores[0].start()
    for c in range(2):
        fetch[c].wait()
        field = up[c]
        add = jnp.dot(refl[last], field, preferred_element_type=F32)
        done[c] = (field.astype(F32) + add * factor).astype(BF16)
        store = pltpu.make_async_copy(done.at[c], src_out.at[c], out_sem.at[c])
        store.start()
        stores.append(store)
        for i in range(1 + c, len(moves), 2):
            loads[i].wait()
            stores[i].start()
    for store in stores:
        store.wait()


def per_device(source_field, data_field, propagator, band_start, freq_slot):
    tile = source_field.shape[2]
    shots = source_field.shape[3]
    band = propagator.shape[4]
    lat_count = lax.axis_size("lat")
    freq_total = source_field.shape[1] * lax.axis_size("freq")
    count_x = freq_total // 2
    sub = tile // 2 // count_x
    reach = round_up(3 * tile, 256)
    vmem = pltpu.VMEM
    dma = pltpu.SemaphoreType.DMA
    field = jax.ShapeDtypeStruct((2, tile, shots), BF16)
    whole = jax.ShapeDtypeStruct((LEVELS, tile, tile), BF16)
    refl, up, dat = pl.pallas_call(
        functools.partial(migrate, lat_count, freq_total),
        out_shape=(whole, field, field),
        in_specs=[pl.BlockSpec(memory_space=pltpu.SMEM)] * 2 + [pl.BlockSpec(memory_space=pl.ANY)] * 3,
        out_specs=[pl.BlockSpec(memory_space=pl.ANY)] * 3,
        scratch_shapes=[
            vmem((LEVELS, 2, tile, band), BF16),
            vmem((LEVELS, 2, tile, 2 * reach), BF16),
            vmem((LEVELS, 2, 2, reach, shots), BF16),
            vmem((2, reach, shots), BF16),
            vmem((2, 2, tile, shots), BF16),
            vmem((LEVELS, 2, count_x, sub, tile), F32),
            vmem((LEVELS, count_x, sub, tile), F32),
            vmem((LEVELS, count_x - 1, sub, tile), BF16),
            vmem((LEVELS, count_x - 1, sub, tile), BF16),
            vmem((4, 2, count_x, sub, tile), BF16),
            vmem((4, tile, tile), BF16),
            vmem((tile if sub % 16 else 8, tile), F32),
            dma((2,)),
            dma((2,)),
            dma((4,)),
            dma((LEVELS, 4, 2)),
            dma((LEVELS, 4, 2)),
            dma((LEVELS, count_x)),
            dma((LEVELS, count_x)),
            dma((LEVELS, count_x - 1)),
            dma((LEVELS, count_x - 1)),
            dma((4, count_x - 1)),
            dma((4, count_x - 1)),
            dma((4, count_x)),
            dma((4, count_x)),
            dma((2,)),
            dma((2,)),
        ],
        compiler_params=pltpu.CompilerParams(
            collective_id=0, has_side_effects=True, vmem_limit_bytes=60 * 1024 * 1024
        ),
    )(
        band_start[:, 0],
        freq_slot,
        source_field[:, 0],
        data_field[:, 0],
        propagator[:, :, 0],
    )
    refl, src, dat = pl.pallas_call(
        finish,
        out_shape=(whole, field, field),
        in_specs=[pl.BlockSpec(memory_space=pl.ANY)] * 3,
        out_specs=[pl.BlockSpec(memory_space=pl.ANY)] * 3,
        scratch_shapes=[
            vmem((LEVELS, tile, tile), BF16),
            vmem((2, tile, shots), BF16),
            vmem((2, tile, shots), BF16),
            vmem((2, tile, shots), BF16),
            dma((4 + LEVELS,)),
            dma((4 + LEVELS,)),
        ],
    )(refl, up, dat)
    return refl, src[:, None], dat[:, None]


def solution(mesh):
    return jax.shard_map(
        per_device,
        mesh=mesh,
        in_specs=(
            P("grp", "freq", "lat", None),
            P("grp", "freq", "lat", None),
            P("grp", None, "freq", "lat", None),
            P("grp", "lat"),
            P("freq"),
        ),
        out_specs=(
            P("grp", "lat", None),
            P("grp", "freq", "lat", None),
            P("grp", "freq", "lat", None),
        ),
        check_vma=False,
    )
```
